128 devices in a mesh: side: 2 (over z_lo), group: 2 (over z_hi), shard: 32 (over x, y, core).
Axes of the slice: x: 4, y: 4, z: 4 (z_hi: 2, z_lo: 2; z = z_hi * 2 + z_lo), core: 2. Of those that a mesh axis runs over, the one named last changes fastest.
Arguments:
- grad_parts: bfloat16 [4, 4, 7168, 2048], P(('side', 'group'), None, 'shard'), may hold values from -6 to 6
- master: float32 [4, 7168, 2048], P(('side', 'group'), 'shard'), may hold values from -6 to 6
- moment: float32 [4, 7168, 2048], P(('side', 'group'), 'shard'), may hold values from -4 to 4
- variance: float32 [4, 7168, 2048], P(('side', 'group'), 'shard'), may hold values from 0.0004 to 0.04
- plan: int32 [4], replicated, may hold values from 0 to 3, each once
- step: int32 [4], replicated, may hold values from 1 to 16
Outputs:
- new_master: float32 [4, 7168, 2048], P(('side', 'group'), 'shard')
- new_moment: float32 [4, 7168, 2048], P(('side', 'group'), 'shard')
- new_variance: float32 [4, 7168, 2048], P(('side', 'group'), 'shard')
- rollout_weights: bfloat16 [4, 2048, 7168], P(None, 'shard')
The draws below stay inside these ranges and needn't reach their ends.
Inputs may be any that keep to these rules, and one draw needn't show every extreme that they name: `plan`: a permutation of the slots; slot s belongs to owner group s (groups numbered side-major).
All inputs are finite; a program needn't handle non-finite values.
Results may differ from the reference program's by a relative error of at most 0.0075.
Values may be sent and summed in bfloat16 or wider, within the bound.
A program may use at most 128 MiB of HBM per device.

```python
import math
import jax
import jax.numpy as jnp

D = 7168
F = 2048
GROUPS = 4
NB = 4


def with_ends(drawn, stream_key, least, top_value):
    spot = [jax.random.randint(jax.random.fold_in(stream_key, axis), (), 0, length) for axis, length in enumerate(drawn.shape)]
    main_axis = drawn.shape.index(max(drawn.shape))
    next_to = spot[:main_axis] + [(spot[main_axis] + 1) % drawn.shape[main_axis]] + spot[main_axis + 1:]
    return drawn.at[tuple(spot)].set(least).at[tuple(next_to)].set(top_value)


def shard_levels(key, dims, split, smallest, largest):
    gain = 1.0
    for position, blocks in split:
        steps = jax.random.uniform(jax.random.fold_in(jax.random.fold_in(key, 6), position), (blocks,), jnp.float32, smallest / len(split), largest / len(split))
        gain = gain * jnp.repeat(jnp.exp(steps), dims[position] // blocks).reshape((-1,) + (1,) * (len(dims) - 1 - position))
    return gain


def noise(rng, extent, deviation, reach, split=(), held_as=jnp.bfloat16):
    array = jax.random.normal(rng, extent, jnp.float32) * deviation
    if len(split) > 0:
        array = shard_levels(rng, extent, split, -0.22, 0.18) * array
    return jnp.clip(array, min=-reach, max=reach).astype(held_as)


def setup_inputs(seed: int = 0) -> dict:
    key_of = jax.random.split(jax.random.key(seed), 7)
    return {
        "grad_parts": noise(key_of[0], (GROUPS, NB, D, F), 1.0, 6.0, ((0, 4), (2, 32))),
        "master": noise(key_of[1], (NB, D, F), 1.0, 6.0, ((0, 4), (1, 32)), jnp.float32),
        "moment": noise(key_of[2], (NB, D, F), 0.5, 4.0, ((0, 4), (1, 32)), jnp.float32),
        "variance": jnp.clip(jnp.exp(math.log(0.04) - 4.6051702 * jax.random.uniform(key_of[3], (NB, D, F), jnp.float32) ** shard_levels(key_of[3], (NB, D, F), ((0, 4), (1, 32)), -0.2, 0.2)), 0.0004, 0.04),
        "plan": jax.random.permutation(key_of[4], NB).astype(jnp.int32),
        "step": with_ends(jax.random.randint(key_of[5], (NB,), 1, 17), jax.random.fold_in(key_of[5], 1), 1, 16).astype(jnp.int32),
    }


BETA_ONE = 0.9
BETA_TWO = 0.999
LEARN = 0.1
DECAY = 0.1
EPSILON = 1e-08

def reference(grad_parts, master, moment, variance, plan, step):
    grad = jnp.zeros(master.shape, jnp.float32)
    for index in range(GROUPS):
        grad = grad + grad_parts[index].astype(jnp.float32)
    counting = jnp.arange(NB, dtype=jnp.int32)
    matrix_of_slot = jnp.zeros((NB,), jnp.int32).at[plan].set(counting)
    slotted = grad[matrix_of_slot]
    new_moment = BETA_ONE * moment + (1.0 - BETA_ONE) * slotted
    new_variance = BETA_TWO * variance + (1.0 - BETA_TWO) * slotted * slotted
    count = step[matrix_of_slot].astype(jnp.float32)[:, None, None]
    first_fix = 1.0 - jnp.power(jnp.float32(BETA_ONE), count)
    second_fix = 1.0 - jnp.power(jnp.float32(BETA_TWO), count)
    update = new_moment / first_fix / (jnp.sqrt(new_variance / second_fix) + EPSILON)
    new_master = master - LEARN * (update + DECAY * master)
    rounded = new_master.astype(jnp.bfloat16)
    rollout_weights = jnp.swapaxes(rounded[plan], 1, 2)
    return (new_master, new_moment, new_variance, rollout_weights)
```

```python
import functools

import jax
import jax.numpy as jnp
from jax import lax
from jax.experimental import pallas as pl
from jax.experimental.pallas import tpu as pltpu
from jax.sharding import PartitionSpec as P

BETA_ONE = 0.9
BETA_TWO = 0.999
LEARN = 0.1
DECAY = 0.1
EPSILON = 1e-08

ROWS = 224
COLS = 2048
HALF = COLS // 2
PIECE = 32
STEPS = ROWS // PIECE
WIDE = 64
LANE = 128
SHARDS = 32
NB = 4
MERGED = 24
MSG = 4
AHEAD = 2
MESH = pl.DeviceIdType.MESH
BF16 = jnp.bfloat16
F32 = jnp.float32


def power(base, count):
    result = jnp.float32(1.0)
    square = base
    for bit in range(5):
        factor = jnp.where((count & (1 << bit)) != 0, jnp.float32(square), jnp.float32(1.0))
        result = result * factor
        square = square * square
    return result


def main_kernel(
    plan, step, grad_hbm, master_hbm, moment_hbm, variance_hbm,
    new_master, new_moment, new_variance, rollout,
    grad, master, moment, variance,
    to_opposite, to_right, to_left, relay_left, relay_right, from_left, from_right,
    turned, parts, whole, mixed,
    load_sem, s_sem, relay_sem, raw_sem, sum_sem, s_raw_sem, s_sum_sem,
    x_send, x_recv, g_send, g_recv,
):
    side, group, shard = lax.axis_index("side"), lax.axis_index("group"), lax.axis_index("shard")
    z = group * 2 + side
    turn = lax.rem(shard, 4)

    def place(other_z, other_shard):
        return (lax.rem(other_z, 2), other_z // 2, other_shard)

    def slot_of(other_z):
        return lax.rem(other_z, 2) * 2 + other_z // 2

    z_right, z_left, z_far = lax.rem(z + 1, 4), lax.rem(z + 3, 4), lax.rem(z + 2, 4)
    right, left = place(z_right, shard), place(z_left, shard)
    mine, slot_right, slot_left, slot_far = slot_of(z), slot_of(z_right), slot_of(z_left), slot_of(z_far)

    loads = [
        pltpu.make_async_copy(grad_hbm, grad, load_sem.at[0]),
        pltpu.make_async_copy(master_hbm, master, load_sem.at[1]),
        pltpu.make_async_copy(moment_hbm, moment, load_sem.at[2]),
        pltpu.make_async_copy(variance_hbm, variance, load_sem.at[3]),
    ]
    for load in loads:
        load.start()

    barrier = pltpu.get_barrier_semaphore()
    pl.semaphore_signal(barrier, inc=1, device_id=right, device_id_type=MESH)
    pl.semaphore_signal(barrier, inc=1, device_id=left, device_id_type=MESH)

    def greet(offset, carry):
        other = lax.rem(shard + offset, SHARDS)
        pl.semaphore_signal(barrier, inc=1, device_id=place(z, other), device_id_type=MESH)
        return carry

    lax.fori_loop(1, SHARDS, greet, 0)

    def matrix_of(slot):
        found = jnp.int32(0)
        for b in range(1, NB):
            found = jnp.where(plan[b] == slot, jnp.int32(b), found)
        return found

    b_mine, b_right, b_left, b_far = matrix_of(mine), matrix_of(slot_right), matrix_of(slot_left), matrix_of(slot_far)
    count = step[b_mine]
    one = jnp.ones((1, LANE), F32)
    first_scale = one / (one * (1.0 - power(BETA_ONE, count)))
    second_scale = one / (one * (1.0 - power(BETA_TWO, count)))

    loads[0].wait()
    pl.semaphore_wait(barrier, SHARDS + 1)

    def rows_at(position):
        segment = lax.rem(turn + position, 8)
        return pl.multiple_of(jnp.minimum(segment, STEPS - 1) * PIECE, PIECE)

    def rows_of(index):
        position = index + jnp.where(index >= STEPS - turn, 1, 0)
        return pl.ds(rows_at(position), PIECE)

    low, high = pl.ds(0, HALF), pl.ds(HALF, HALF)

    def remote(src, dst, send, recv, where):
        return pltpu.make_async_remote_copy(
            src_ref=src, dst_ref=dst, send_sem=send, recv_sem=recv, device_id=where, device_id_type=MESH
        )

    def relays(i):
        rows = rows_of(i)
        return (
            remote(to_opposite.at[rows, low], relay_left.at[rows, :], s_sem.at[i, 0], relay_sem.at[i, 0], right),
            remote(to_opposite.at[rows, high], relay_right.at[rows, :], s_sem.at[i, 1], relay_sem.at[i, 1], left),
        )

    def raws(i):
        rows = rows_of(i)
        return (
            remote(to_right.at[rows, high], from_left.at[rows, high], s_raw_sem.at[i, 0], raw_sem.at[i, 0], right),
            remote(to_left.at[rows, low], from_right.at[rows, low], s_raw_sem.at[i, 1], raw_sem.at[i, 1], left),
        )

    def sums(i):
        rows = rows_of(i)
        return (
            remote(to_right.at[rows, low], from_left.at[rows, low], s_sum_sem.at[i, 0], sum_sem.at[i, 0], right),
            remote(to_left.at[rows, high], from_right.at[rows, high], s_sum_sem.at[i, 1], sum_sem.at[i, 1], left),
        )

    def begin(i):
        rows = rows_of(i)
        to_opposite[rows, :] = grad[b_far, rows, :]
        to_right[rows, high] = grad[b_right, rows, high]
        to_left[rows, low] = grad[b_left, rows, low]
        for copy in relays(i) + raws(i):
            copy.start()

    def add(i):
        rows = rows_of(i)
        first, second = relays(i)
        to_r, to_l = sums(i)
        first.wait_recv()
        own = grad[b_right, rows, low].astype(F32)
        to_right[rows, low] = (relay_left[rows, :].astype(F32) + own).astype(BF16)
        to_r.start()
        second.wait_recv()
        own = grad[b_left, rows, high].astype(F32)
        to_left[rows, high] = (relay_right[rows, :].astype(F32) + own).astype(BF16)
        to_l.start()

    def update(i):
        rows = rows_of(i)
        for copy in raws(i) + sums(i):
            copy.wait_recv()

        def tile(j, carry):
            lanes = pl.ds(pl.multiple_of(j * LANE, LANE), LANE)
            total = (
                grad[b_mine, rows, lanes].astype(F32)
                + from_left[rows, lanes].astype(F32)
                + from_right[rows, lanes].astype(F32)
            )
            first = BETA_ONE * moment[rows, lanes] + (1.0 - BETA_ONE) * total
            second = BETA_TWO * variance[rows, lanes] + (1.0 - BETA_TWO) * total * total
            old = master[rows, lanes]
            change = (first * first_scale) / (jnp.sqrt(second * second_scale) + EPSILON)
            new_moment[rows, lanes] = first
            new_variance[rows, lanes] = second
            new_master[rows, lanes] = old - LEARN * (change + DECAY * old)
            return carry

        lax.fori_loop(0, COLS // LANE, tile, 0)

    def exchange(phase, landing):
        my_chip, core = shard // 2, lax.rem(shard, 2)

        def turn_chip(chip):
            lanes = pl.ds(pl.multiple_of(chip * LANE, LANE), LANE)
            block = jnp.concatenate(
                [new_master[pl.ds(rows_at(4 * phase + q), PIECE), lanes] for q in range(4)], axis=0
            )
            turned[phase, pl.ds(pl.multiple_of(chip * LANE, LANE), LANE), :] = block.T.astype(BF16)

        def source(other):
            return turned.at[phase, pl.ds(pl.multiple_of(other * WIDE, WIDE), WIDE), :]

        def send(other):
            remote(source(other), landing(shard), x_send.at[phase], x_recv.at[phase], place(z, other)).start()

        turn_chip(my_chip)

        def one(k, carry):
            turn_chip(lax.rem(my_chip + k, SHARDS // 2))

            @pl.when(k > 1)
            def _():
                before = lax.rem(my_chip + k - 1, SHARDS // 2)
                send(before * 2)
                send(before * 2 + 1)

            return carry

        lax.fori_loop(1, SHARDS // 2, one, 0)
        last = lax.rem(my_chip + SHARDS // 2 - 1, SHARDS // 2)
        send(last * 2)
        send(last * 2 + 1)
        send(my_chip * 2 + 1 - core)
        landing(shard)[...] = turned[phase, pl.ds(pl.multiple_of(shard * WIDE, WIDE), WIDE), :]

    def exchanged(phase, landing):
        everything = landing(pl.ds(0, SHARDS - 1))
        remote(everything, everything, x_send.at[phase], x_recv.at[phase], right).wait_recv()

    def gather_copies(phase, buffer, size, slot, way, m, kind):
        where = right if way == 0 else left
        part = buffer.at[slot, pl.ds(m * size, size)]
        return remote(part, part, g_send.at[phase, kind, way, m], g_recv.at[phase, kind, way, m], where)

    ORDER = ((0, 1, 2, 3), (2, 3, 0, 1))
    def gather_own(phase, buffer, size):
        for k in range(MSG):
            for way in range(2):
                gather_copies(phase, buffer, size, mine, way, ORDER[way][k], 0).start()

    def gather_forward(phase, buffer, size):
        for k in range(MSG // 2):
            for way in range(2):
                m = ORDER[way][k]
                slot = slot_left if way == 0 else slot_right
                gather_copies(phase, buffer, size, slot, way, m, 0).wait_recv()
                gather_copies(phase, buffer, size, slot, way, m, 1).start()

    def gathered(phase, buffer, size):
        for k in range(MSG // 2, MSG):
            for way in range(2):
                slot = slot_left if way == 0 else slot_right
                gather_copies(phase, buffer, size, slot, way, ORDER[way][k], 0).wait_recv()
        for k in range(MSG // 2):
            for way in range(2):
                gather_copies(phase, buffer, size, slot_far, way, ORDER[way][k], 1).wait_recv()

    def land_whole(source):
        return parts.at[mine, source]

    def land_mixed(source):
        return mixed.at[source]

    for i in range(AHEAD):
        begin(jnp.int32(i))
    for load in loads[1:]:
        load.wait()
    for i in range(STEPS):
        if i + AHEAD < STEPS:
            begin(jnp.int32(i + AHEAD))
        add(jnp.int32(i))
        if i >= 1:
            update(jnp.int32(i - 1))
        if i == 4:
            exchange(0, land_whole)
    exchanged(0, land_whole)
    gather_own(0, parts, 32 // MSG)
    update(jnp.int32(STEPS - 1))
    exchange(1, land_mixed)
    gather_forward(0, parts, 32 // MSG)
    exchanged(1, land_mixed)

    lane = lax.broadcasted_iota(jnp.int32, (WIDE, LANE), 1)

    def merge(g, carry):
        for a in range(3):
            whole[mine, 3 * g + a] = jnp.where(
                lane < LANE - PIECE - PIECE * a, mixed[4 * g + a], mixed[4 * g + a + 1]
            )
        return carry

    lax.fori_loop(0, 8, merge, 0)
    gather_own(1, whole, MERGED // MSG)
    gathered(0, parts, 32 // MSG)

    def put_parts(g, carry):
        for b in range(NB):
            for a in range(4):
                lanes = pl.ds(pl.multiple_of((7 * g + 2 * a) * LANE, LANE), LANE)
                rollout[b, :, lanes] = parts[plan[b], 4 * g + a]
        return carry

    lax.fori_loop(0, 8, put_parts, 0)
    gather_forward(1, whole, MERGED // MSG)
    gathered(1, whole, MERGED // MSG)

    def put_whole(g, carry):
        for b in range(NB):
            for a in range(3):
                lanes = pl.ds(pl.multiple_of((7 * g + 2 * a + 1) * LANE, LANE), LANE)
                rollout[b, :, lanes] = whole[plan[b], 3 * g + a]
        return carry

    lax.fori_loop(0, 8, put_whole, 0)

    for i in range(STEPS):
        for copy in relays(jnp.int32(i)) + raws(jnp.int32(i)) + sums(jnp.int32(i)):
            copy.wait_send()
    for phase, landing in ((0, land_whole), (1, land_mixed)):
        everything = landing(pl.ds(0, SHARDS - 1))
        remote(everything, everything, x_send.at[phase], x_recv.at[phase], right).wait_send()
    for phase, buffer, size in ((0, parts, 32 // MSG), (1, whole, MERGED // MSG)):
        for k in range(MSG):
            for way in range(2):
                gather_copies(phase, buffer, size, mine, way, ORDER[way][k], 0).wait_send()
        for k in range(MSG // 2):
            for way in range(2):
                slot = slot_left if way == 0 else slot_right
                gather_copies(phase, buffer, size, slot, way, ORDER[way][k], 1).wait_send()


def write_kernel(*refs):
    sources, results, sems = refs[:4], refs[4:8], refs[8]
    copies = [pltpu.make_async_copy(s, r, sems.at[i]) for i, (s, r) in enumerate(zip(sources, results))]
    for copy in copies:
        copy.start()
    for copy in copies:
        copy.wait()


def body(grad_parts, master, moment, variance, plan, step):
    hbm = pl.BlockSpec(memory_space=pltpu.HBM)
    vmem = pl.BlockSpec(memory_space=pltpu.VMEM)
    smem = pl.BlockSpec(memory_space=pltpu.SMEM)
    state = jax.ShapeDtypeStruct((ROWS, COLS), F32)
    outs = [state, state, state, jax.ShapeDtypeStruct((NB, WIDE, SHARDS * ROWS), BF16)]
    dma = pltpu.SemaphoreType.DMA
    results = pl.pallas_call(
        main_kernel,
        out_shape=outs,
        in_specs=[smem, smem] + [hbm] * 4,
        out_specs=[vmem] * 4,
        scratch_shapes=[
            pltpu.VMEM((NB, ROWS, COLS), BF16),
            pltpu.VMEM((ROWS, COLS), F32),
            pltpu.VMEM((ROWS, COLS), F32),
            pltpu.VMEM((ROWS, COLS), F32),
            pltpu.VMEM((ROWS, COLS), BF16),
            pltpu.VMEM((ROWS, COLS), BF16),
            pltpu.VMEM((ROWS, COLS), BF16),
            pltpu.VMEM((ROWS, HALF), BF16),
            pltpu.VMEM((ROWS, HALF), BF16),
            pltpu.VMEM((ROWS, COLS), BF16),
            pltpu.VMEM((ROWS, COLS), BF16),
            pltpu.VMEM((2, COLS, LANE), BF16),
            pltpu.VMEM((NB, SHARDS, WIDE, LANE), BF16),
            pltpu.VMEM((NB, MERGED, WIDE, LANE), BF16),
            pltpu.VMEM((SHARDS, WIDE, LANE), BF16),
            dma((4,)),
            dma((STEPS, 2)),
            dma((STEPS, 2)),
            dma((STEPS, 2)),
            dma((STEPS, 2)),
            dma((STEPS, 2)),
            dma((STEPS, 2)),
            dma((2,)),
            dma((2,)),
            dma((2, 2, 2, MSG)),
            dma((2, 2, 2, MSG)),
        ],
        compiler_params=pltpu.CompilerParams(
            collective_id=0, has_side_effects=True, vmem_limit_bytes=26 << 20
        ),
        name="update_and_hand_off",
    )(plan, step, *[pltpu.with_memory_space_constraint(x[0], pltpu.HBM) for x in (grad_parts, master, moment, variance)])
    new_master, new_moment, new_variance, rollout = pl.pallas_call(
        write_kernel,
        out_shape=outs,
        in_specs=[vmem] * 4,
        out_specs=[hbm] * 4,
        scratch_shapes=[dma((4,))],
        compiler_params=pltpu.CompilerParams(vmem_limit_bytes=16 << 20),
        name="write_results",
    )(*results)
    return (new_master[None], new_moment[None], new_variance[None], rollout)


def solution(mesh):
    return jax.shard_map(
        body,
        mesh=mesh,
        in_specs=(
            P(("side", "group"), None, "shard", None),
            P(("side", "group"), "shard", None),
            P(("side", "group"), "shard", None),
            P(("side", "group"), "shard", None),
            P(),
            P(),
        ),
        out_specs=(
            P(("side", "group"), "shard", None),
            P(("side", "group"), "shard", None),
            P(("side", "group"), "shard", None),
            P(None, "shard", None),
        ),
        check_vma=False,
    )
```

```python
import functools

import jax
import jax.numpy as jnp
from jax import lax
from jax.experimental import pallas as pl
from jax.experimental.pallas import tpu as pltpu
from jax.sharding import PartitionSpec as P

BETA_ONE = 0.9
BETA_TWO = 0.999
LEARN = 0.1
DECAY = 0.1
EPSILON = 1e-08

ROWS = 224
COLS = 2048
HALF = COLS // 2
PIECE = 32
STEPS = ROWS // PIECE
EARLY = 2
WIDE = 64
LANE = 128
SHARDS = 32
NB = 4
MERGED = 24
MSG = 4
MESH = pl.DeviceIdType.MESH
BF16 = jnp.bfloat16
F32 = jnp.float32


def power(base, count):
    result = jnp.float32(1.0)
    square = base
    for bit in range(5):
        factor = jnp.where((count & (1 << bit)) != 0, jnp.float32(square), jnp.float32(1.0))
        result = result * factor
        square = square * square
    return result


def main_kernel(
    plan_hbm, step_hbm, grad_hbm, master_hbm, moment_hbm, variance_hbm,
    new_master, new_moment, new_variance, rollout,
    plan, step, grad, early, master, moment, variance,
    to_opposite, to_right, to_left, relay_left, relay_right, from_left, from_right,
    turned, parts, whole, mixed,
    load_sem, plane_sem, s_sem, relay_sem, raw_sem, sum_sem, s_raw_sem, s_sum_sem,
    x_send, x_recv, g_send, g_recv,
):
    side, group, shard = lax.axis_index("side"), lax.axis_index("group"), lax.axis_index("shard")
    z = group * 2 + side
    turn = lax.rem(shard, 4)

    def place(other_z, other_shard):
        return (lax.rem(other_z, 2), other_z // 2, other_shard)

    def slot_of(other_z):
        return lax.rem(other_z, 2) * 2 + other_z // 2

    z_right, z_left, z_far = lax.rem(z + 1, 4), lax.rem(z + 3, 4), lax.rem(z + 2, 4)
    right, left = place(z_right, shard), place(z_left, shard)
    mine, slot_right, slot_left, slot_far = slot_of(z), slot_of(z_right), slot_of(z_left), slot_of(z_far)

    fetches = [
        pltpu.make_async_copy(plan_hbm, plan, load_sem.at[4]),
        pltpu.make_async_copy(step_hbm, step, load_sem.at[5]),
        pltpu.make_async_copy(
            grad_hbm.at[:, pl.ds(pl.multiple_of(turn * PIECE, PIECE), EARLY * PIECE), :], early, load_sem.at[6]
        ),
    ]
    loads = [
        pltpu.make_async_copy(grad_hbm, grad, load_sem.at[0]),
        pltpu.make_async_copy(master_hbm, master, load_sem.at[1]),
        pltpu.make_async_copy(moment_hbm, moment, load_sem.at[2]),
        pltpu.make_async_copy(variance_hbm, variance, load_sem.at[3]),
    ]
    for load in fetches + loads:
        load.start()

    row, column = shard // 8, lax.rem(shard, 8)
    across = [place(z, lax.rem(row + k, 4) * 8 + column) for k in range(1, 4)]
    barrier = pltpu.get_barrier_semaphore()
    for other in [right, left] + across + [place(z, row * 8 + lax.rem(column + k, 8)) for k in range(1, 8)]:
        pl.semaphore_signal(barrier, inc=1, device_id=other, device_id_type=MESH)

    for load in fetches:
        load.wait()

    def matrix_of(slot):
        found = jnp.int32(0)
        for b in range(1, NB):
            found = jnp.where(plan[b] == slot, jnp.int32(b), found)
        return found

    b_mine, b_right, b_left, b_far = matrix_of(mine), matrix_of(slot_right), matrix_of(slot_left), matrix_of(slot_far)
    count = step[b_mine]
    one = jnp.ones((1, LANE), F32)
    first_scale = one / (one * (1.0 - power(BETA_ONE, count)))
    second_scale = one / (one * (1.0 - power(BETA_TWO, count)))

    def rows_at(position):
        segment = lax.rem(turn + position, 8)
        return pl.multiple_of(jnp.minimum(segment, STEPS - 1) * PIECE, PIECE)

    def rows_of(index):
        position = index + jnp.where(index >= STEPS - turn, 1, 0)
        return pl.ds(rows_at(position), PIECE)

    low, high = pl.ds(0, HALF), pl.ds(HALF, HALF)

    def remote(src, dst, send, recv, where):
        return pltpu.make_async_remote_copy(
            src_ref=src, dst_ref=dst, send_sem=send, recv_sem=recv, device_id=where, device_id_type=MESH
        )

    def relays(i):
        rows = rows_of(i)
        return (
            remote(to_opposite.at[rows, low], relay_left.at[rows, :], s_sem.at[i, 0], relay_sem.at[i, 0], right),
            remote(to_opposite.at[rows, high], relay_right.at[rows, :], s_sem.at[i, 1], relay_sem.at[i, 1], left),
        )

    def raws(i):
        rows = rows_of(i)
        return (
            remote(to_right.at[rows, high], from_left.at[rows, high], s_raw_sem.at[i, 0], raw_sem.at[i, 0], right),
            remote(to_left.at[rows, low], from_right.at[rows, low], s_raw_sem.at[i, 1], raw_sem.at[i, 1], left),
        )

    def sums(i):
        rows = rows_of(i)
        return (
            remote(to_right.at[rows, low], from_left.at[rows, low], s_sum_sem.at[i, 0], sum_sem.at[i, 0], right),
            remote(to_left.at[rows, high], from_right.at[rows, high], s_sum_sem.at[i, 1], sum_sem.at[i, 1], left),
        )

    def staged(i):
        return (early, pl.ds(i * PIECE, PIECE)) if i < EARLY else (grad, rows_of(jnp.int32(i)))

    def stage_relays(i):
        source, at = staged(i)
        to_opposite[rows_of(jnp.int32(i)), :] = source[b_far, at, :]

    def stage_raws(i):
        source, at = staged(i)
        to_right[rows_of(jnp.int32(i)), high] = source[b_right, at, high]
        to_left[rows_of(jnp.int32(i)), low] = source[b_left, at, low]

    def start(copies):
        for copy in copies:
            copy.start()

    def add(i):
        rows = rows_of(i)
        first, second = relays(i)
        to_r, to_l = sums(i)
        first.wait_recv()
        own = grad[b_right, rows, low].astype(F32)
        to_right[rows, low] = (relay_left[rows, :].astype(F32) + own).astype(BF16)
        to_r.start()
        second.wait_recv()
        own = grad[b_left, rows, high].astype(F32)
        to_left[rows, high] = (relay_right[rows, :].astype(F32) + own).astype(BF16)
        to_l.start()

    def update(i):
        rows = rows_of(i)
        for copy in raws(i) + sums(i):
            copy.wait_recv()

        def tile(j, carry):
            lanes = pl.ds(pl.multiple_of(j * LANE, LANE), LANE)
            total = (
                grad[b_mine, rows, lanes].astype(F32)
                + from_left[rows, lanes].astype(F32)
                + from_right[rows, lanes].astype(F32)
            )
            first = BETA_ONE * moment[rows, lanes] + (1.0 - BETA_ONE) * total
            second = BETA_TWO * variance[rows, lanes] + (1.0 - BETA_TWO) * total * total
            old = master[rows, lanes]
            change = (first * first_scale) / (jnp.sqrt(second * second_scale) + EPSILON)
            new_moment[rows, lanes] = first
            new_variance[rows, lanes] = second
            new_master[rows, lanes] = old - LEARN * (change + DECAY * old)
            return carry

        lax.fori_loop(0, COLS // LANE, tile, 0)

    def exchange(phase, landing):
        my_chip, core = shard // 2, lax.rem(shard, 2)

        def turn_chip(chip):
            lanes = pl.ds(pl.multiple_of(chip * LANE, LANE), LANE)
            block = jnp.concatenate(
                [new_master[pl.ds(rows_at(4 * phase + q), PIECE), lanes] for q in range(4)], axis=0
            )
            turned[phase, pl.ds(pl.multiple_of(chip * LANE, LANE), LANE), :] = block.T.astype(BF16)

        def source(other):
            return turned.at[phase, pl.ds(pl.multiple_of(other * WIDE, WIDE), WIDE), :]

        def send(other):
            remote(source(other), landing(shard), x_send.at[phase], x_recv.at[phase], place(z, other)).start()

        turn_chip(my_chip)

        def one(k, carry):
            turn_chip(lax.rem(my_chip + k, SHARDS // 2))

            @pl.when(k > 1)
            def _():
                before = lax.rem(my_chip + k - 1, SHARDS // 2)
                send(before * 2)
                send(before * 2 + 1)

            return carry

        lax.fori_loop(1, SHARDS // 2, one, 0)
        last = lax.rem(my_chip + SHARDS // 2 - 1, SHARDS // 2)
        send(last * 2)
        send(last * 2 + 1)
        send(my_chip * 2 + 1 - core)
        landing(shard)[...] = turned[phase, pl.ds(pl.multiple_of(shard * WIDE, WIDE), WIDE), :]

    def exchanged(phase, landing):
        everything = landing(pl.ds(0, SHARDS - 1))
        remote(everything, everything, x_send.at[phase], x_recv.at[phase], right).wait_recv()

    def gather_copies(phase, buffer, size, slot, way, m, kind):
        where = right if way == 0 else left
        part = buffer.at[slot, pl.ds(m * size, size)]
        return remote(part, part, g_send.at[phase, kind, way, m], g_recv.at[phase, kind, way, m], where)

    ORDER = ((0, 1, 2, 3), (2, 3, 0, 1))
    def gather_own(phase, buffer, size):
        for k in range(MSG):
            for way in range(2):
                gather_copies(phase, buffer, size, mine, way, ORDER[way][k], 0).start()

    def gather_forward(phase, buffer, size):
        for k in range(MSG // 2):
            for way in range(2):
                m = ORDER[way][k]
                slot = slot_left if way == 0 else slot_right
                gather_copies(phase, buffer, size, slot, way, m, 0).wait_recv()
                gather_copies(phase, buffer, size, slot, way, m, 1).start()

    def gathered(phase, buffer, size):
        for k in range(MSG // 2, MSG):
            for way in range(2):
                slot = slot_left if way == 0 else slot_right
                gather_copies(phase, buffer, size, slot, way, ORDER[way][k], 0).wait_recv()
        for k in range(MSG // 2):
            for way in range(2):
                gather_copies(phase, buffer, size, slot_far, way, ORDER[way][k], 1).wait_recv()

    def land_whole(source):
        return parts.at[mine, source]

    def land_mixed(source):
        return mixed.at[source]

    stage_relays(0)
    stage_raws(0)
    pl.semaphore_wait(barrier, 12)
    start(relays(jnp.int32(0)) + raws(jnp.int32(0)))
    for other in across:
        pl.semaphore_signal(plane_sem, inc=1, device_id=other, device_id_type=MESH)
    for i in range(STEPS):
        if i + 1 < STEPS:
            stage_relays(i + 1)
            start(relays(jnp.int32(i + 1)))
        if i == 0:
            loads[0].wait()
        add(jnp.int32(i))
        if i + 1 < STEPS:
            stage_raws(i + 1)
            start(raws(jnp.int32(i + 1)))
        if i == 1:
            for load in loads[1:]:
                load.wait()
            pl.semaphore_wait(plane_sem, 3)
        if 1 <= i < STEPS - 1:
            update(jnp.int32(i - 1))
        if i == 4:
            exchange(0, land_whole)
    exchanged(0, land_whole)
    gather_own(0, parts, 32 // MSG)
    update(jnp.int32(STEPS - 2))
    update(jnp.int32(STEPS - 1))
    exchange(1, land_mixed)
    gather_forward(0, parts, 32 // MSG)
    exchanged(1, land_mixed)

    lane = lax.broadcasted_iota(jnp.int32, (WIDE, LANE), 1)

    def merge(g, carry):
        for a in range(3):
            whole[mine, 3 * g + a] = jnp.where(
                lane < LANE - PIECE - PIECE * a, mixed[4 * g + a], mixed[4 * g + a + 1]
            )
        return carry

    lax.fori_loop(0, 8, merge, 0)
    gather_own(1, whole, MERGED // MSG)
    for i in range(STEPS):
        for copy in relays(jnp.int32(i)) + raws(jnp.int32(i)) + sums(jnp.int32(i)):
            copy.wait_send()
    for phase, landing in ((0, land_whole), (1, land_mixed)):
        everything = landing(pl.ds(0, SHARDS - 1))
        remote(everything, everything, x_send.at[phase], x_recv.at[phase], right).wait_send()
    gathered(0, parts, 32 // MSG)

    def put_parts(g, carry):
        for b in range(NB):
            for a in range(4):
                lanes = pl.ds(pl.multiple_of((7 * g + 2 * a) * LANE, LANE), LANE)
                rollout[b, :, lanes] = parts[plan[b], 4 * g + a]
        return carry

    lax.fori_loop(0, 8, put_parts, 0)
    gather_forward(1, whole, MERGED // MSG)
    gathered(1, whole, MERGED // MSG)

    def put_whole(g, carry):
        for b in range(NB):
            for a in range(3):
                lanes = pl.ds(pl.multiple_of((7 * g + 2 * a + 1) * LANE, LANE), LANE)
                rollout[b, :, lanes] = whole[plan[b], 3 * g + a]
        return carry

    lax.fori_loop(0, 8, put_whole, 0)

    for phase, buffer, size in ((0, parts, 32 // MSG), (1, whole, MERGED // MSG)):
        for k in range(MSG):
            for way in range(2):
                gather_copies(phase, buffer, size, mine, way, ORDER[way][k], 0).wait_send()
        for k in range(MSG // 2):
            for way in range(2):
                slot = slot_left if way == 0 else slot_right
                gather_copies(phase, buffer, size, slot, way, ORDER[way][k], 1).wait_send()


def write_kernel(*refs):
    sources, results, sems = refs[:4], refs[4:8], refs[8]
    copies = [pltpu.make_async_copy(s, r, sems.at[i]) for i, (s, r) in enumerate(zip(sources, results))]
    for copy in copies:
        copy.start()
    for copy in copies:
        copy.wait()


def body(grad_parts, master, moment, variance, plan, step):
    hbm = pl.BlockSpec(memory_space=pltpu.HBM)
    vmem = pl.BlockSpec(memory_space=pltpu.VMEM)
    state = jax.ShapeDtypeStruct((ROWS, COLS), F32)
    outs = [state, state, state, jax.ShapeDtypeStruct((NB, WIDE, SHARDS * ROWS), BF16)]
    dma = pltpu.SemaphoreType.DMA
    results = pl.pallas_call(
        main_kernel,
        out_shape=outs,
        in_specs=[hbm] * 6,
        out_specs=[vmem] * 4,
        scratch_shapes=[
            pltpu.SMEM((NB,), jnp.int32),
            pltpu.SMEM((NB,), jnp.int32),
            pltpu.VMEM((NB, ROWS, COLS), BF16),
            pltpu.VMEM((NB, EARLY * PIECE, COLS), BF16),
            pltpu.VMEM((ROWS, COLS), F32),
            pltpu.VMEM((ROWS, COLS), F32),
            pltpu.VMEM((ROWS, COLS), F32),
            pltpu.VMEM((ROWS, COLS), BF16),
            pltpu.VMEM((ROWS, COLS), BF16),
            pltpu.VMEM((ROWS, COLS), BF16),
            pltpu.VMEM((ROWS, HALF), BF16),
            pltpu.VMEM((ROWS, HALF), BF16),
            pltpu.VMEM((ROWS, COLS), BF16),
            pltpu.VMEM((ROWS, COLS), BF16),
            pltpu.VMEM((2, COLS, LANE), BF16),
            pltpu.VMEM((NB, SHARDS, WIDE, LANE), BF16),
            pltpu.VMEM((NB, MERGED, WIDE, LANE), BF16),
            pltpu.VMEM((SHARDS, WIDE, LANE), BF16),
            dma((7,)),
            pltpu.SemaphoreType.REGULAR,
            dma((STEPS, 2)),
            dma((STEPS, 2)),
            dma((STEPS, 2)),
            dma((STEPS, 2)),
            dma((STEPS, 2)),
            dma((STEPS, 2)),
            dma((2,)),
            dma((2,)),
            dma((2, 2, 2, MSG)),
            dma((2, 2, 2, MSG)),
        ],
        compiler_params=pltpu.CompilerParams(
            collective_id=0, has_side_effects=True, vmem_limit_bytes=28 << 20
        ),
        name="update_and_hand_off",
    )(*[pltpu.with_memory_space_constraint(x, pltpu.HBM) for x in (plan, step, grad_parts[0], master[0], moment[0], variance[0])])
    new_master, new_moment, new_variance, rollout = pl.pallas_call(
        write_kernel,
        out_shape=outs,
        in_specs=[vmem] * 4,
        out_specs=[hbm] * 4,
        scratch_shapes=[dma((4,))],
        compiler_params=pltpu.CompilerParams(vmem_limit_bytes=16 << 20),
        name="write_results",
    )(*results)
    return (new_master[None], new_moment[None], new_variance[None], rollout)


def solution(mesh):
    return jax.shard_map(
        body,
        mesh=mesh,
        in_specs=(
            P(("side", "group"), None, "shard", None),
            P(("side", "group"), "shard", None),
            P(("side", "group"), "shard", None),
            P(("side", "group"), "shard", None),
            P(),
            P(),
        ),
        out_specs=(
            P(("side", "group"), "shard", None),
            P(("side", "group"), "shard", None),
            P(("side", "group"), "shard", None),
            P(None, "shard", None),
        ),
        check_vma=False,
    )
```

```python
import functools

import jax
import jax.numpy as jnp
from jax import lax
from jax.experimental import pallas as pl
from jax.experimental.pallas import tpu as pltpu
from jax.sharding import PartitionSpec as P

BETA_ONE = 0.9
BETA_TWO = 0.999
LEARN = 0.1
DECAY = 0.1
EPSILON = 1e-08

ROWS = 224
COLS = 2048
HALF = COLS // 2
PIECE = 32
STEPS = ROWS // PIECE
GROUP = 512
FULL = 4 * PIECE
WIDE = 64
LANE = 128
SHARDS = 32
NB = 4
MERGED = 24
MSG = 4
MESH = pl.DeviceIdType.MESH
BF16 = jnp.bfloat16
F32 = jnp.float32


def power(base, count):
    result = jnp.float32(1.0)
    square = base
    for bit in range(5):
        factor = jnp.where((count & (1 << bit)) != 0, jnp.float32(square), jnp.float32(1.0))
        result = result * factor
        square = square * square
    return result


def main_kernel(
    plan_hbm, step_hbm, grad_hbm, master_hbm, moment_hbm, variance_hbm,
    new_master, new_moment, new_variance, rollout,
    plan, step, grad, early, master, moment, variance,
    to_opposite, to_right, to_left, relay, from_left, from_right,
    turned, parts, whole, mixed,
    load_sem, plane_sem, s_sem, relay_sem, raw_sem, sum_sem, s_raw_sem, s_sum_sem,
    x_send, x_recv, g_send, g_recv,
):
    side, group, shard = lax.axis_index("side"), lax.axis_index("group"), lax.axis_index("shard")
    z = group * 2 + side
    turn = lax.rem(shard, 4)

    def place(other_z, other_shard):
        return (lax.rem(other_z, 2), other_z // 2, other_shard)

    def slot_of(other_z):
        return lax.rem(other_z, 2) * 2 + other_z // 2

    z_right, z_left, z_far = lax.rem(z + 1, 4), lax.rem(z + 3, 4), lax.rem(z + 2, 4)
    right, left = place(z_right, shard), place(z_left, shard)
    mine, slot_right, slot_left, slot_far = slot_of(z), slot_of(z_right), slot_of(z_left), slot_of(z_far)

    row, column = shard // 8, lax.rem(shard, 8)

    def group_of(i):
        return pl.ds(pl.multiple_of(lax.rem(row + i, 4) * GROUP, GROUP), GROUP)

    fetches = [
        pltpu.make_async_copy(plan_hbm, plan, load_sem.at[4]),
        pltpu.make_async_copy(step_hbm, step, load_sem.at[5]),
        pltpu.make_async_copy(
            grad_hbm.at[:, pl.ds(pl.multiple_of(turn * PIECE, PIECE), FULL), group_of(0)], early, load_sem.at[6]
        ),
    ]
    loads = [
        pltpu.make_async_copy(grad_hbm, grad, load_sem.at[0]),
        pltpu.make_async_copy(master_hbm, master, load_sem.at[1]),
        pltpu.make_async_copy(moment_hbm, moment, load_sem.at[2]),
        pltpu.make_async_copy(variance_hbm, variance, load_sem.at[3]),
    ]
    for load in fetches + loads:
        load.start()

    along = [place(z, row * 8 + lax.rem(column + k, 8)) for k in range(1, 8)]
    across = [place(z, lax.rem(row + k, 4) * 8 + column) for k in range(1, 4)]
    barrier = pltpu.get_barrier_semaphore()

    def signal(semaphore, others):
        for other in others:
            pl.semaphore_signal(semaphore, inc=1, device_id=other, device_id_type=MESH)

    signal(barrier, [right, left])

    @pl.when(z == 0)
    def _():
        signal(barrier, along)

    @pl.when(z == 1)
    def _():
        signal(barrier, across)

    def tell(stage):
        if stage == 0:

            @pl.when(z == 1)
            def _():
                signal(plane_sem.at[0], [left])

        if stage == 1:

            @pl.when(z == 0)
            def _():
                pl.semaphore_wait(plane_sem.at[0], 1)
                signal(plane_sem.at[1], along)

        if stage == 2:

            @pl.when(z == 0)
            def _():
                pl.semaphore_wait(plane_sem.at[1], 7)
                signal(plane_sem.at[2], [right])

        if stage == 3:

            @pl.when(z == 1)
            def _():
                pl.semaphore_wait(plane_sem.at[2], 1)
                signal(plane_sem.at[3], across)

        if stage == 4:

            @pl.when(z == 1)
            def _():
                pl.semaphore_wait(plane_sem.at[3], 3)
                signal(plane_sem.at[4], [left, right])

        if stage == 5:

            @pl.when(z == 0)
            def _():
                pl.semaphore_wait(plane_sem.at[4], 1)

            @pl.when(z == 2)
            def _():
                pl.semaphore_wait(plane_sem.at[4], 1)
                signal(plane_sem.at[4], [right])

        if stage == 6:

            @pl.when(z == 3)
            def _():
                pl.semaphore_wait(plane_sem.at[4], 1)

    for load in fetches:
        load.wait()

    def matrix_of(slot):
        found = jnp.int32(0)
        for b in range(1, NB):
            found = jnp.where(plan[b] == slot, jnp.int32(b), found)
        return found

    b_mine, b_right, b_left, b_far = matrix_of(mine), matrix_of(slot_right), matrix_of(slot_left), matrix_of(slot_far)
    count = step[b_mine]
    one = jnp.ones((1, LANE), F32)
    first_scale = one / (one * (1.0 - power(BETA_ONE, count)))
    second_scale = one / (one * (1.0 - power(BETA_TWO, count)))

    def rows_at(position):
        segment = lax.rem(turn + position, 8)
        return pl.multiple_of(jnp.minimum(segment, STEPS - 1) * PIECE, PIECE)

    def rows_of(i):
        if i < 4:
            return pl.ds(pl.multiple_of(turn * PIECE, PIECE), FULL)
        return pl.ds(rows_at(i + jnp.where(i >= STEPS - turn, 1, 0)), PIECE)

    def half(i, k):
        if i < 4:
            first = lax.rem(row + i, 4) * GROUP + k * (GROUP // 2)
            return rows_of(i), pl.ds(pl.multiple_of(first, GROUP // 2), GROUP // 2)
        return rows_of(i), pl.ds(k * HALF, HALF)

    def remote(src, dst, send, recv, where):
        return pltpu.make_async_remote_copy(
            src_ref=src, dst_ref=dst, send_sem=send, recv_sem=recv, device_id=where, device_id_type=MESH
        )

    def relays(i):
        low, high = half(i, 0), half(i, 1)
        return (
            remote(to_opposite.at[low], relay.at[low], s_sem.at[i, 0], relay_sem.at[i, 0], right),
            remote(to_opposite.at[high], relay.at[high], s_sem.at[i, 1], relay_sem.at[i, 1], left),
        )

    def raws(i):
        low, high = half(i, 0), half(i, 1)
        return (
            remote(to_right.at[high], from_left.at[high], s_raw_sem.at[i, 0], raw_sem.at[i, 0], right),
            remote(to_left.at[low], from_right.at[low], s_raw_sem.at[i, 1], raw_sem.at[i, 1], left),
        )

    def sums(i):
        low, high = half(i, 0), half(i, 1)
        return (
            remote(to_right.at[low], from_left.at[low], s_sum_sem.at[i, 0], sum_sem.at[i, 0], right),
            remote(to_left.at[high], from_right.at[high], s_sum_sem.at[i, 1], sum_sem.at[i, 1], left),
        )

    def part_of(b, i, k):
        if i == 0:
            return early[b, :, pl.ds(k * (GROUP // 2), GROUP // 2)]
        rows, lanes = half(i, k)
        return grad[b, rows, lanes]

    def stage_relays(i):
        for k in range(2):
            to_opposite[half(i, k)] = part_of(b_far, i, k)

    def stage_raws(i):
        to_right[half(i, 1)] = part_of(b_right, i, 1)
        to_left[half(i, 0)] = part_of(b_left, i, 0)

    def start(copies):
        for copy in copies:
            copy.start()

    def add(i):
        low, high = half(i, 0), half(i, 1)
        first, second = relays(i)
        to_r, to_l = sums(i)
        first.wait_recv()
        to_right[low] = (relay[low].astype(F32) + part_of(b_right, i, 0).astype(F32)).astype(BF16)
        to_r.start()
        second.wait_recv()
        to_left[high] = (relay[high].astype(F32) + part_of(b_left, i, 1).astype(F32)).astype(BF16)
        to_l.start()

    def update(i):
        for copy in raws(i) + sums(i):
            copy.wait_recv()

        def tile(j, carry):
            if i < 4:
                rows = pl.ds(pl.multiple_of((turn + j // 4) * PIECE, PIECE), PIECE)
                lanes = pl.ds(pl.multiple_of(lax.rem(row + i, 4) * GROUP + lax.rem(j, 4) * LANE, LANE), LANE)
            else:
                rows, lanes = rows_of(i), pl.ds(pl.multiple_of(j * LANE, LANE), LANE)
            total = (
                grad[b_mine, rows, lanes].astype(F32)
                + from_left[rows, lanes].astype(F32)
                + from_right[rows, lanes].astype(F32)
            )
            first = BETA_ONE * moment[rows, lanes] + (1.0 - BETA_ONE) * total
            second = BETA_TWO * variance[rows, lanes] + (1.0 - BETA_TWO) * total * total
            old = master[rows, lanes]
            change = (first * first_scale) / (jnp.sqrt(second * second_scale) + EPSILON)
            new_moment[rows, lanes] = first
            new_variance[rows, lanes] = second
            new_master[rows, lanes] = old - LEARN * (change + DECAY * old)
            return carry

        lax.fori_loop(0, COLS // LANE, tile, 0)

    def exchange(phase, landing, i):
        first = lax.rem(row + i, 4) * 4
        my_chip = lax.rem(shard, 8) // 2

        def turn_chip(chip):
            lanes = pl.ds(pl.multiple_of(chip * LANE, LANE), LANE)
            block = jnp.concatenate(
                [new_master[pl.ds(rows_at(4 * phase + q), PIECE), lanes] for q in range(4)], axis=0
            )
            turned[phase, lanes, :] = block.T.astype(BF16)

        def source(other):
            return turned.at[phase, pl.ds(pl.multiple_of(other * WIDE, WIDE), WIDE), :]

        def send(other):
            remote(source(other), landing(shard), x_send.at[phase], x_recv.at[phase], place(z, other)).start()

        def send_chip(k):
            if i == 0 and k == 0:
                send(shard + 1 - 2 * lax.rem(shard, 2))
            else:
                chip = first + lax.rem(my_chip + k, 4)
                send(chip * 2)
                send(chip * 2 + 1)

        for k in range(4):
            turn_chip(first + lax.rem(my_chip + k, 4))
            if k > 0:
                send_chip(k - 1)
        send_chip(3)
        if i == 0:
            landing(shard)[...] = turned[phase, pl.ds(pl.multiple_of(shard * WIDE, WIDE), WIDE), :]

    def exchanged(phase, landing):
        everything = landing(pl.ds(0, SHARDS - 1))
        remote(everything, everything, x_send.at[phase], x_recv.at[phase], right).wait_recv()

    def gather_copies(phase, buffer, size, slot, way, m, kind):
        where = right if way == 0 else left
        part = buffer.at[slot, pl.ds(m * size, size)]
        return remote(part, part, g_send.at[phase, kind, way, m], g_recv.at[phase, kind, way, m], where)

    ORDER = ((0, 1, 2, 3), (2, 3, 0, 1))
    def gather_own(phase, buffer, size):
        for k in range(MSG):
            for way in range(2):
                gather_copies(phase, buffer, size, mine, way, ORDER[way][k], 0).start()

    def gather_forward(phase, buffer, size):
        for k in range(MSG // 2):
            for way in range(2):
                m = ORDER[way][k]
                slot = slot_left if way == 0 else slot_right
                gather_copies(phase, buffer, size, slot, way, m, 0).wait_recv()
                gather_copies(phase, buffer, size, slot, way, m, 1).start()

    def gathered(phase, buffer, size):
        for k in range(MSG // 2, MSG):
            for way in range(2):
                slot = slot_left if way == 0 else slot_right
                gather_copies(phase, buffer, size, slot, way, ORDER[way][k], 0).wait_recv()
        for k in range(MSG // 2):
            for way in range(2):
                gather_copies(phase, buffer, size, slot_far, way, ORDER[way][k], 1).wait_recv()

    def land_whole(source):
        return parts.at[mine, source]

    def land_mixed(source):
        return mixed.at[source]

    stage_relays(0)
    stage_raws(0)
    pl.semaphore_wait(barrier, 2 + jnp.where(z == 0, 7, 0) + jnp.where(z == 1, 3, 0))
    start(relays(0) + raws(0))
    tell(0)
    for i in range(STEPS):
        if i == 0:
            loads[0].wait()
        if i + 1 < STEPS:
            stage_relays(i + 1)
            start(relays(i + 1))
        if i == 1:
            tell(2)
        if i == 2:
            tell(5)
        add(i)
        if i + 1 < STEPS:
            stage_raws(i + 1)
            start(raws(i + 1))
        if i == 0:
            tell(1)
        if i == 1:
            tell(3)
        if i == 2:
            tell(6)
        if i == 1:
            for load in loads[1:]:
                load.wait()
        if 1 <= i < STEPS - 1:
            update(i - 1)
        if i == 1:
            tell(4)
        if 2 <= i <= 4:
            for k in range(0 if i == 2 else i - 1, i):
                exchange(0, land_whole, k)
    exchanged(0, land_whole)
    gather_own(0, parts, 32 // MSG)
    update(STEPS - 2)
    update(STEPS - 1)
    for i in range(4):
        exchange(1, land_mixed, i)
    gather_forward(0, parts, 32 // MSG)
    exchanged(1, land_mixed)

    lane = lax.broadcasted_iota(jnp.int32, (WIDE, LANE), 1)

    def merge(g, carry):
        for a in range(3):
            whole[mine, 3 * g + a] = jnp.where(
                lane < LANE - PIECE - PIECE * a, mixed[4 * g + a], mixed[4 * g + a + 1]
            )
        return carry

    lax.fori_loop(0, 8, merge, 0)
    gather_own(1, whole, MERGED // MSG)
    for i in range(STEPS):
        for copy in relays(i) + raws(i) + sums(i):
            copy.wait_send()
    for phase, landing in ((0, land_whole), (1, land_mixed)):
        everything = landing(pl.ds(0, SHARDS - 1))
        remote(everything, everything, x_send.at[phase], x_recv.at[phase], right).wait_send()
    gathered(0, parts, 32 // MSG)

    def put_parts(g, carry):
        for b in range(NB):
            for a in range(4):
                lanes = pl.ds(pl.multiple_of((7 * g + 2 * a) * LANE, LANE), LANE)
                rollout[b, :, lanes] = parts[plan[b], 4 * g + a]
        return carry

    lax.fori_loop(0, 8, put_parts, 0)
    gather_forward(1, whole, MERGED // MSG)
    gathered(1, whole, MERGED // MSG)

    def put_whole(g, carry):
        for b in range(NB):
            for a in range(3):
                lanes = pl.ds(pl.multiple_of((7 * g + 2 * a + 1) * LANE, LANE), LANE)
                rollout[b, :, lanes] = whole[plan[b], 3 * g + a]
        return carry

    lax.fori_loop(0, 8, put_whole, 0)

    for phase, buffer, size in ((0, parts, 32 // MSG), (1, whole, MERGED // MSG)):
        for k in range(MSG):
            for way in range(2):
                gather_copies(phase, buffer, size, mine, way, ORDER[way][k], 0).wait_send()
        for k in range(MSG // 2):
            for way in range(2):
                slot = slot_left if way == 0 else slot_right
                gather_copies(phase, buffer, size, slot, way, ORDER[way][k], 1).wait_send()


def write_kernel(*refs):
    sources, results, sems = refs[:4], refs[4:8], refs[8]
    copies = [pltpu.make_async_copy(s, r, sems.at[i]) for i, (s, r) in enumerate(zip(sources, results))]
    for copy in copies:
        copy.start()
    for copy in copies:
        copy.wait()


def body(grad_parts, master, moment, variance, plan, step):
    hbm = pl.BlockSpec(memory_space=pltpu.HBM)
    vmem = pl.BlockSpec(memory_space=pltpu.VMEM)
    state = jax.ShapeDtypeStruct((ROWS, COLS), F32)
    outs = [state, state, state, jax.ShapeDtypeStruct((NB, WIDE, SHARDS * ROWS), BF16)]
    dma = pltpu.SemaphoreType.DMA
    results = pl.pallas_call(
        main_kernel,
        out_shape=outs,
        in_specs=[hbm] * 6,
        out_specs=[vmem] * 4,
        scratch_shapes=[
            pltpu.SMEM((NB,), jnp.int32),
            pltpu.SMEM((NB,), jnp.int32),
            pltpu.VMEM((NB, ROWS, COLS), BF16),
            pltpu.VMEM((NB, FULL, GROUP), BF16),
            pltpu.VMEM((ROWS, COLS), F32),
            pltpu.VMEM((ROWS, COLS), F32),
            pltpu.VMEM((ROWS, COLS), F32),
            pltpu.VMEM((ROWS, COLS), BF16),
            pltpu.VMEM((ROWS, COLS), BF16),
            pltpu.VMEM((ROWS, COLS), BF16),
            pltpu.VMEM((ROWS, COLS), BF16),
            pltpu.VMEM((ROWS, COLS), BF16),
            pltpu.VMEM((ROWS, COLS), BF16),
            pltpu.VMEM((2, COLS, LANE), BF16),
            pltpu.VMEM((NB, SHARDS, WIDE, LANE), BF16),
            pltpu.VMEM((NB, MERGED, WIDE, LANE), BF16),
            pltpu.VMEM((SHARDS, WIDE, LANE), BF16),
            dma((7,)),
            pltpu.SemaphoreType.REGULAR((5,)),
            dma((STEPS, 2)),
            dma((STEPS, 2)),
            dma((STEPS, 2)),
            dma((STEPS, 2)),
            dma((STEPS, 2)),
            dma((STEPS, 2)),
            dma((2,)),
            dma((2,)),
            dma((2, 2, 2, MSG)),
            dma((2, 2, 2, MSG)),
        ],
        compiler_params=pltpu.CompilerParams(
            collective_id=0, has_side_effects=True, vmem_limit_bytes=28 << 20
        ),
        name="update_and_hand_off",
    )(*[pltpu.with_memory_space_constraint(x, pltpu.HBM) for x in (plan, step, grad_parts[0], master[0], moment[0], variance[0])])
    new_master, new_moment, new_variance, rollout = pl.pallas_call(
        write_kernel,
        out_shape=outs,
        in_specs=[vmem] * 4,
        out_specs=[hbm] * 4,
        scratch_shapes=[dma((4,))],
        compiler_params=pltpu.CompilerParams(vmem_limit_bytes=16 << 20),
        name="write_results",
    )(*results)
    return (new_master[None], new_moment[None], new_variance[None], rollout)


def solution(mesh):
    return jax.shard_map(
        body,
        mesh=mesh,
        in_specs=(
            P(("side", "group"), None, "shard", None),
            P(("side", "group"), "shard", None),
            P(("side", "group"), "shard", None),
            P(("side", "group"), "shard", None),
            P(),
            P(),
        ),
        out_specs=(
            P(("side", "group"), "shard", None),
            P(("side", "group"), "shard", None),
            P(("side", "group"), "shard", None),
            P(None, "shard", None),
        ),
        check_vma=False,
    )
```

```python
import functools

import jax
import jax.numpy as jnp
from jax import lax
from jax.experimental import pallas as pl
from jax.experimental.pallas import tpu as pltpu
from jax.sharding import PartitionSpec as P

BETA_ONE = 0.9
BETA_TWO = 0.999
LEARN = 0.1
DECAY = 0.1
EPSILON = 1e-08

ROWS = 224
COLS = 2048
HALF = COLS // 2
PIECE = 32
STEPS = ROWS // PIECE
GROUP = 512
FULL = 4 * PIECE
WIDE = 64
LANE = 128
SHARDS = 32
NB = 4
MERGED = 24
MSG = 4
MESH = pl.DeviceIdType.MESH
BF16 = jnp.bfloat16
F32 = jnp.float32


def power(base, count):
    result = jnp.float32(1.0)
    square = base
    for bit in range(5):
        factor = jnp.where((count & (1 << bit)) != 0, jnp.float32(square), jnp.float32(1.0))
        result = result * factor
        square = square * square
    return result


def main_kernel(
    plan_hbm, step_hbm, grad_hbm, master_hbm, moment_hbm, variance_hbm,
    new_master, new_moment, new_variance, parts, whole,
    plan, step, grad, early, master, moment, variance,
    to_opposite, to_right, to_left, relay, from_left, from_right,
    turned, mixed,
    load_sem, plane_sem, s_sem, relay_sem, raw_sem, sum_sem, s_raw_sem, s_sum_sem,
    x_send, x_recv, g_send, g_recv,
):
    side, group, shard = lax.axis_index("side"), lax.axis_index("group"), lax.axis_index("shard")
    z = group * 2 + side
    turn = lax.rem(shard, 4)

    def place(other_z, other_shard):
        return (lax.rem(other_z, 2), other_z // 2, other_shard)

    def slot_of(other_z):
        return lax.rem(other_z, 2) * 2 + other_z // 2

    z_right, z_left, z_far = lax.rem(z + 1, 4), lax.rem(z + 3, 4), lax.rem(z + 2, 4)
    right, left = place(z_right, shard), place(z_left, shard)
    mine, slot_right, slot_left, slot_far = slot_of(z), slot_of(z_right), slot_of(z_left), slot_of(z_far)

    row, column = shard // 8, lax.rem(shard, 8)

    def group_of(i):
        return pl.ds(pl.multiple_of(lax.rem(row + i, 4) * GROUP, GROUP), GROUP)

    fetches = [
        pltpu.make_async_copy(plan_hbm, plan, load_sem.at[4]),
        pltpu.make_async_copy(step_hbm, step, load_sem.at[5]),
        pltpu.make_async_copy(
            grad_hbm.at[:, pl.ds(pl.multiple_of(turn * PIECE, PIECE), FULL), group_of(0)], early, load_sem.at[6]
        ),
    ]
    loads = [
        pltpu.make_async_copy(grad_hbm, grad, load_sem.at[0]),
        pltpu.make_async_copy(master_hbm, master, load_sem.at[1]),
        pltpu.make_async_copy(moment_hbm, moment, load_sem.at[2]),
        pltpu.make_async_copy(variance_hbm, variance, load_sem.at[3]),
    ]
    for load in fetches:
        load.start()

    along = [place(z, row * 8 + lax.rem(column + k, 8)) for k in range(1, 8)]
    across = [place(z, lax.rem(row + k, 4) * 8 + column) for k in range(1, 4)]
    barrier = pltpu.get_barrier_semaphore()

    def signal(semaphore, others):
        for other in others:
            pl.semaphore_signal(semaphore, inc=1, device_id=other, device_id_type=MESH)

    signal(barrier, [right, left])

    @pl.when(z == 0)
    def _():
        signal(barrier, along)

    @pl.when(z == 1)
    def _():
        signal(barrier, across)

    def tell(stage):
        if stage == 0:

            @pl.when(z == 1)
            def _():
                signal(plane_sem.at[0], [left])

        if stage == 1:

            @pl.when(z == 0)
            def _():
                pl.semaphore_wait(plane_sem.at[0], 1)
                signal(plane_sem.at[1], along)

        if stage == 2:

            @pl.when(z == 0)
            def _():
                pl.semaphore_wait(plane_sem.at[1], 7)
                signal(plane_sem.at[2], [right])

        if stage == 3:

            @pl.when(z == 1)
            def _():
                pl.semaphore_wait(plane_sem.at[2], 1)
                signal(plane_sem.at[3], across)

        if stage == 4:

            @pl.when(z == 1)
            def _():
                pl.semaphore_wait(plane_sem.at[3], 3)
                signal(plane_sem.at[4], [left, right])

        if stage == 5:

            @pl.when(z == 0)
            def _():
                pl.semaphore_wait(plane_sem.at[4], 1)

            @pl.when(z == 2)
            def _():
                pl.semaphore_wait(plane_sem.at[4], 1)
                signal(plane_sem.at[4], [right])

        if stage == 6:

            @pl.when(z == 3)
            def _():
                pl.semaphore_wait(plane_sem.at[4], 1)

    for load in fetches:
        load.wait()
    for load in loads:
        load.start()

    def matrix_of(slot):
        found = jnp.int32(0)
        for b in range(1, NB):
            found = jnp.where(plan[b] == slot, jnp.int32(b), found)
        return found

    b_mine, b_right, b_left, b_far = matrix_of(mine), matrix_of(slot_right), matrix_of(slot_left), matrix_of(slot_far)

    def rows_at(position):
        segment = lax.rem(turn + position, 8)
        return pl.multiple_of(jnp.minimum(segment, STEPS - 1) * PIECE, PIECE)

    def rows_of(i):
        if i < 4:
            return pl.ds(pl.multiple_of(turn * PIECE, PIECE), FULL)
        return pl.ds(rows_at(i + jnp.where(i >= STEPS - turn, 1, 0)), PIECE)

    def half(i, k):
        if i < 4:
            first = lax.rem(row + i, 4) * GROUP + k * (GROUP // 2)
            return rows_of(i), pl.ds(pl.multiple_of(first, GROUP // 2), GROUP // 2)
        return rows_of(i), pl.ds(k * HALF, HALF)

    def remote(src, dst, send, recv, where):
        return pltpu.make_async_remote_copy(
            src_ref=src, dst_ref=dst, send_sem=send, recv_sem=recv, device_id=where, device_id_type=MESH
        )

    def relays(i):
        low, high = half(i, 0), half(i, 1)
        return (
            remote(to_opposite.at[low], relay.at[low], s_sem.at[i, 0], relay_sem.at[i, 0], right),
            remote(to_opposite.at[high], relay.at[high], s_sem.at[i, 1], relay_sem.at[i, 1], left),
        )

    def raws(i):
        low, high = half(i, 0), half(i, 1)
        return (
            remote(to_right.at[high], from_left.at[high], s_raw_sem.at[i, 0], raw_sem.at[i, 0], right),
            remote(to_left.at[low], from_right.at[low], s_raw_sem.at[i, 1], raw_sem.at[i, 1], left),
        )

    def sums(i):
        low, high = half(i, 0), half(i, 1)
        return (
            remote(to_right.at[low], from_left.at[low], s_sum_sem.at[i, 0], sum_sem.at[i, 0], right),
            remote(to_left.at[high], from_right.at[high], s_sum_sem.at[i, 1], sum_sem.at[i, 1], left),
        )

    def part_of(b, i, k):
        if i == 0:
            return early[b, :, pl.ds(k * (GROUP // 2), GROUP // 2)]
        rows, lanes = half(i, k)
        return grad[b, rows, lanes]

    def stage_relays(i):
        for k in range(2):
            to_opposite[half(i, k)] = part_of(b_far, i, k)

    def stage_raws(i):
        to_right[half(i, 1)] = part_of(b_right, i, 1)
        to_left[half(i, 0)] = part_of(b_left, i, 0)

    def start(copies):
        for copy in copies:
            copy.start()

    def add(i):
        low, high = half(i, 0), half(i, 1)
        first, second = relays(i)
        to_r, to_l = sums(i)
        first.wait_recv()
        to_right[low] = (relay[low].astype(F32) + part_of(b_right, i, 0).astype(F32)).astype(BF16)
        to_r.start()
        second.wait_recv()
        to_left[high] = (relay[high].astype(F32) + part_of(b_left, i, 1).astype(F32)).astype(BF16)
        to_l.start()

    def update(i):
        for copy in raws(i) + sums(i):
            copy.wait_recv()

        def tile(j, carry):
            if i < 4:
                rows = pl.ds(pl.multiple_of((turn + j // 4) * PIECE, PIECE), PIECE)
                lanes = pl.ds(pl.multiple_of(lax.rem(row + i, 4) * GROUP + lax.rem(j, 4) * LANE, LANE), LANE)
            else:
                rows, lanes = rows_of(i), pl.ds(pl.multiple_of(j * LANE, LANE), LANE)
            total = (
                grad[b_mine, rows, lanes].astype(F32)
                + from_left[rows, lanes].astype(F32)
                + from_right[rows, lanes].astype(F32)
            )
            first = BETA_ONE * moment[rows, lanes] + (1.0 - BETA_ONE) * total
            second = BETA_TWO * variance[rows, lanes] + (1.0 - BETA_TWO) * total * total
            old = master[rows, lanes]
            change = (first * first_scale) / (jnp.sqrt(second * second_scale) + EPSILON)
            new_moment[rows, lanes] = first
            new_variance[rows, lanes] = second
            new_master[rows, lanes] = old - LEARN * (change + DECAY * old)
            return carry

        lax.fori_loop(0, COLS // LANE, tile, 0)

    def exchange(phase, landing, i):
        first = lax.rem(row + i, 4) * 4
        my_chip = lax.rem(shard, 8) // 2

        def turn_chip(chip):
            lanes = pl.ds(pl.multiple_of(chip * LANE, LANE), LANE)
            block = jnp.concatenate(
                [new_master[pl.ds(rows_at(4 * phase + q), PIECE), lanes] for q in range(4)], axis=0
            )
            turned[phase, lanes, :] = block.T.astype(BF16)

        def source(other):
            return turned.at[phase, pl.ds(pl.multiple_of(other * WIDE, WIDE), WIDE), :]

        def send(other):
            remote(source(other), landing(shard), x_send.at[phase], x_recv.at[phase], place(z, other)).start()

        def send_chip(k):
            if i == 0 and k == 0:
                send(shard + 1 - 2 * lax.rem(shard, 2))
            else:
                chip = first + lax.rem(my_chip + k, 4)
                send(chip * 2)
                send(chip * 2 + 1)

        for k in range(4):
            turn_chip(first + lax.rem(my_chip + k, 4))
            if k > 0:
                send_chip(k - 1)
        send_chip(3)
        if i == 0:
            landing(shard)[...] = turned[phase, pl.ds(pl.multiple_of(shard * WIDE, WIDE), WIDE), :]

    def exchanged(phase, landing):
        everything = landing(pl.ds(0, SHARDS - 1))
        remote(everything, everything, x_send.at[phase], x_recv.at[phase], right).wait_recv()

    def gather_copies(phase, buffer, size, slot, way, m, kind):
        where = right if way == 0 else left
        part = buffer.at[slot, pl.ds(m * size, size)]
        return remote(part, part, g_send.at[phase, kind, way, m], g_recv.at[phase, kind, way, m], where)

    ORDER = ((0, 1, 2, 3), (2, 3, 0, 1))
    def gather_own(phase, buffer, size):
        for k in range(MSG):
            for way in range(2):
                gather_copies(phase, buffer, size, mine, way, ORDER[way][k], 0).start()

    def gather_forward(phase, buffer, size):
        for k in range(MSG // 2):
            for way in range(2):
                m = ORDER[way][k]
                slot = slot_left if way == 0 else slot_right
                gather_copies(phase, buffer, size, slot, way, m, 0).wait_recv()
                gather_copies(phase, buffer, size, slot, way, m, 1).start()

    def gathered(phase, buffer, size):
        for k in range(MSG // 2, MSG):
            for way in range(2):
                slot = slot_left if way == 0 else slot_right
                gather_copies(phase, buffer, size, slot, way, ORDER[way][k], 0).wait_recv()
        for k in range(MSG // 2):
            for way in range(2):
                gather_copies(phase, buffer, size, slot_far, way, ORDER[way][k], 1).wait_recv()

    def land_whole(source):
        return parts.at[mine, source]

    def land_mixed(source):
        return mixed.at[source]

    stage_relays(0)
    pl.semaphore_wait(barrier, 2 + jnp.where(z == 0, 7, 0) + jnp.where(z == 1, 3, 0))
    start(relays(0))
    stage_raws(0)
    start(raws(0))
    tell(0)
    count = step[b_mine]
    one = jnp.ones((1, LANE), F32)
    first_scale = one / (one * (1.0 - power(BETA_ONE, count)))
    second_scale = one / (one * (1.0 - power(BETA_TWO, count)))
    for i in range(STEPS):
        if i == 0:
            loads[0].wait()
        if i + 1 < STEPS:
            stage_relays(i + 1)
            start(relays(i + 1))
        if i == 1:
            tell(2)
        if i == 2:
            tell(5)
        add(i)
        if i + 1 < STEPS:
            stage_raws(i + 1)
            start(raws(i + 1))
        if i == 0:
            tell(1)
        if i == 1:
            tell(3)
        if i == 2:
            tell(6)
        if i == 1:
            for load in loads[1:]:
                load.wait()
        if 1 <= i < STEPS - 1:
            update(i - 1)
        if i == 1:
            tell(4)
        if 2 <= i <= 4:
            for k in range(0 if i == 2 else i - 1, i):
                exchange(0, land_whole, k)
    exchanged(0, land_whole)
    gather_own(0, parts, 32 // MSG)
    update(STEPS - 2)
    update(STEPS - 1)
    for i in range(4):
        exchange(1, land_mixed, i)
    gather_forward(0, parts, 32 // MSG)
    exchanged(1, land_mixed)

    lane = lax.broadcasted_iota(jnp.int32, (WIDE, LANE), 1)

    def merge(g, carry):
        for a in range(3):
            whole[mine, 3 * g + a] = jnp.where(
                lane < LANE - PIECE - PIECE * a, mixed[4 * g + a], mixed[4 * g + a + 1]
            )
        return carry

    lax.fori_loop(0, 8, merge, 0)
    gather_own(1, whole, MERGED // MSG)
    for i in range(STEPS):
        for copy in relays(i) + raws(i) + sums(i):
            copy.wait_send()
    for phase, landing in ((0, land_whole), (1, land_mixed)):
        everything = landing(pl.ds(0, SHARDS - 1))
        remote(everything, everything, x_send.at[phase], x_recv.at[phase], right).wait_send()
    gathered(0, parts, 32 // MSG)

    gather_forward(1, whole, MERGED // MSG)
    gathered(1, whole, MERGED // MSG)

    for phase, buffer, size in ((0, parts, 32 // MSG), (1, whole, MERGED // MSG)):
        for k in range(MSG):
            for way in range(2):
                gather_copies(phase, buffer, size, mine, way, ORDER[way][k], 0).wait_send()
        for k in range(MSG // 2):
            for way in range(2):
                slot = slot_left if way == 0 else slot_right
                gather_copies(phase, buffer, size, slot, way, ORDER[way][k], 1).wait_send()


def write_kernel(
    plan_hbm, master_in, moment_in, variance_in, parts, whole,
    master, moment, variance, rollout, plan, plan_sem, sems,
):
    fetch = pltpu.make_async_copy(plan_hbm, plan, plan_sem)
    fetch.start()
    states = [
        pltpu.make_async_copy(source, result, sems.at[i])
        for i, (source, result) in enumerate(((master_in, master), (moment_in, moment), (variance_in, variance)))
    ]
    for copy in states:
        copy.start()
    fetch.wait()

    def start(source, b, block):
        lanes = pl.ds(pl.multiple_of(block * LANE, LANE), LANE)
        pltpu.make_async_copy(source, rollout.at[b, :, lanes], sems.at[4]).start()

    def group(g, carry):
        for b in range(NB):
            slot = plan[b]
            for a in range(4):
                start(parts.at[slot, 4 * g + a], b, 7 * g + 2 * a)
        for b in range(NB):
            slot = plan[b]
            for a in range(3):
                start(whole.at[slot, 3 * g + a], b, 7 * g + 2 * a + 1)
        return carry

    lax.fori_loop(0, 8, group, 0)
    for copy in states:
        copy.wait()
    pltpu.make_async_copy(whole, whole, sems.at[4]).wait()
    pltpu.make_async_copy(parts, parts, sems.at[4]).wait()


def body(grad_parts, master, moment, variance, plan, step):
    hbm = pl.BlockSpec(memory_space=pltpu.HBM)
    vmem = pl.BlockSpec(memory_space=pltpu.VMEM)
    state = jax.ShapeDtypeStruct((ROWS, COLS), F32)
    outs = [state, state, state, jax.ShapeDtypeStruct((NB, WIDE, SHARDS * ROWS), BF16)]
    dma = pltpu.SemaphoreType.DMA
    results = pl.pallas_call(
        main_kernel,
        out_shape=outs[:3] + [jax.ShapeDtypeStruct((NB, SHARDS, WIDE, LANE), BF16), jax.ShapeDtypeStruct((NB, MERGED, WIDE, LANE), BF16)],
        in_specs=[hbm] * 6,
        out_specs=[vmem] * 5,
        scratch_shapes=[
            pltpu.SMEM((NB,), jnp.int32),
            pltpu.SMEM((NB,), jnp.int32),
            pltpu.VMEM((NB, ROWS, COLS), BF16),
            pltpu.VMEM((NB, FULL, GROUP), BF16),
            pltpu.VMEM((ROWS, COLS), F32),
            pltpu.VMEM((ROWS, COLS), F32),
            pltpu.VMEM((ROWS, COLS), F32),
            pltpu.VMEM((ROWS, COLS), BF16),
            pltpu.VMEM((ROWS, COLS), BF16),
            pltpu.VMEM((ROWS, COLS), BF16),
            pltpu.VMEM((ROWS, COLS), BF16),
            pltpu.VMEM((ROWS, COLS), BF16),
            pltpu.VMEM((ROWS, COLS), BF16),
            pltpu.VMEM((2, COLS, LANE), BF16),
            pltpu.VMEM((SHARDS, WIDE, LANE), BF16),
            dma((7,)),
            pltpu.SemaphoreType.REGULAR((5,)),
            dma((STEPS, 2)),
            dma((STEPS, 2)),
            dma((STEPS, 2)),
            dma((STEPS, 2)),
            dma((STEPS, 2)),
            dma((STEPS, 2)),
            dma((2,)),
            dma((2,)),
            dma((2, 2, 2, MSG)),
            dma((2, 2, 2, MSG)),
        ],
        compiler_params=pltpu.CompilerParams(
            collective_id=0, has_side_effects=True, vmem_limit_bytes=28 << 20
        ),
        name="update_and_hand_off",
    )(*[pltpu.with_memory_space_constraint(x, pltpu.HBM) for x in (plan, step, grad_parts[0], master[0], moment[0], variance[0])])
    new_master, new_moment, new_variance, rollout = pl.pallas_call(
        write_kernel,
        out_shape=outs,
        in_specs=[hbm] + [vmem] * 5,
        out_specs=[hbm] * 4,
        scratch_shapes=[pltpu.SMEM((NB,), jnp.int32), dma, dma((5,))],
        compiler_params=pltpu.CompilerParams(vmem_limit_bytes=16 << 20),
        name="write_results",
    )(pltpu.with_memory_space_constraint(plan, pltpu.HBM), *results)
    return (new_master[None], new_moment[None], new_variance[None], rollout)


def solution(mesh):
    return jax.shard_map(
        body,
        mesh=mesh,
        in_specs=(
            P(("side", "group"), None, "shard", None),
            P(("side", "group"), "shard", None),
            P(("side", "group"), "shard", None),
            P(("side", "group"), "shard", None),
            P(),
            P(),
        ),
        out_specs=(
            P(("side", "group"), "shard", None),
            P(("side", "group"), "shard", None),
            P(("side", "group"), "shard", None),
            P(None, "shard", None),
        ),
        check_vma=False,
    )
```
